32 devices in a mesh: gx: 8 (over z, core), gy: 4 (over y, x).
Axes of the slice: x: 2, y: 2, z: 4, core: 2. Of those that a mesh axis runs over, the one named last changes fastest.
Arguments:
- residual: float32 [3, 128, 64, 128], P(None, 'gx', 'gy'), may hold values from -6 to 6
- stiffness: float32 [128, 64], P('gx', 'gy'), may hold values from 0.5 to 2
- local_inverse: bfloat16 [8, 4, 1024, 1024], P('gx', 'gy'), as said below
- coarse_basis: bfloat16 [8, 4, 8, 1024], P('gx', 'gy'), may hold values from -0.5 to 0.5
- coarse_rows: bfloat16 [8, 4, 8, 256], P('gx', 'gy'), as said below
- send_rows: int32 [8, 4, 4, 64], P('gx', 'gy'), may hold values from 0 to 767, as said below
- partition_map: int32 [32], replicated, may hold values from 0 to 31, as said below
Outputs:
- solution: float32 [3, 128, 64, 128], P(None, 'gx', 'gy')
- final: float32 [3, 128, 64, 128], P(None, 'gx', 'gy')
The draws below stay inside these ranges and needn't reach their ends.
Inputs may be any that keep to these rules, and one draw needn't show every extreme that they name: `send_rows`: for each subdomain, the lists j = 0, 1 (lower and upper neighbour along gx) and j = 2, 3 (lower and upper neighbour along gy) each name 64 distinct owned rows, all of them in the two layers of cells nearest that neighbour. `partition_map`: A permutation of the device numbers. `coarse_rows`: with its columns put in device order through partition_map, the 256-square matrix S is symmetric. `local_inverse`: each subdomain's block is symmetric.
All inputs are finite; a program needn't handle non-finite values.
Results may differ from the reference program's by a relative error of at most 0.0057.
Values may be sent and summed in bfloat16 or wider, within the bound.
A program may use at most 64 MiB of HBM per device.

```python
import math
import jax
import jax.numpy as jnp
from jax import lax

NV = 128
CX = 16
CY = 16
OV = 64
K = 8
M = 1024
NX = 128
NY = 64
KD = 256
N_GX = 8
N_GY = 4


def draw_local_inverse(key, part):
    device_count = NX // CX * (NY // CY)
    lower_end, upper_end, spread = (0.12, 0.26, 0.06)

    def one_block(number):
        block_key = jax.random.fold_in(key, number)
        noise_draw = jax.random.normal(jax.random.fold_in(block_key, 1), (M, M), jnp.float32)
        diagonal = jax.random.uniform(jax.random.fold_in(block_key, 2), (M,), jnp.float32, lower_end, upper_end)
        symmetric = (noise_draw + noise_draw.T) * (spread / math.sqrt(2.0 * M))
        return (symmetric + jnp.diag(diagonal)).astype(jnp.bfloat16)
    blocks = lax.map(one_block, jnp.arange(device_count, dtype=jnp.int32))
    return blocks.reshape(NX // CX, NY // CY, M, M)


def coarse_order(key):
    device_count = NX // CX * (NY // CY)
    return jax.random.permutation(jax.random.fold_in(key, 7), device_count).astype(jnp.int32)


def draw_partition_map(key, part):
    return coarse_order(key)


def draw_coarse_rows(key, part):
    device_count = NX // CX * (NY // CY)
    order_size = K * device_count
    back_scale, link_scale = (0.1, 0.25)
    noise_draw = jax.random.normal(jax.random.fold_in(key, 11), (order_size, order_size), jnp.float32)
    background = (noise_draw + noise_draw.T) * (back_scale / math.sqrt(2.0 * order_size))
    diagonal = jax.random.uniform(jax.random.fold_in(key, 12), (order_size,), jnp.float32, 0.1, 0.2)
    partners = jax.random.permutation(jax.random.fold_in(key, 13), device_count)
    first_half = partners[0::2]
    second_half = partners[1::2]
    link_blocks = jax.random.normal(jax.random.fold_in(key, 14), (device_count // 2, K, K), jnp.float32)
    link_blocks = link_blocks * (link_scale / math.sqrt(K))
    pair_terms = jnp.zeros((device_count, K, device_count, K), jnp.float32)
    pair_terms = pair_terms.at[first_half, :, second_half, :].set(link_blocks)
    pair_terms = pair_terms.at[second_half, :, first_half, :].set(jnp.swapaxes(link_blocks, 1, 2))
    whole_matrix = background + pair_terms.reshape(order_size, order_size) + jnp.diag(diagonal)
    positions = coarse_order(key)
    stored = jnp.zeros((order_size, device_count, K), jnp.float32)
    stored = stored.at[:, positions, :].set(whole_matrix.reshape(order_size, device_count, K))
    return stored.astype(jnp.bfloat16).reshape(NX // CX, NY // CY, K, order_size)


def draw_send_rows(key, part):
    device_count = NX // CX * (NY // CY)
    key_list = jax.random.split(key, device_count * 4)
    across_picks = jax.vmap(lambda one_key: jax.random.permutation(one_key, 6 * CY)[:OV])(key_list[:2 * device_count])
    along_picks = jax.vmap(lambda one_key: jax.random.permutation(one_key, 6 * CX)[:OV])(key_list[2 * device_count:])
    across_picks = across_picks.reshape(device_count, 2, OV)
    along_picks = along_picks.reshape(device_count, 2, OV)
    side_index = jnp.arange(2, dtype=jnp.int32)[None, :, None]
    component = across_picks // (2 * CY)
    remainder = across_picks % (2 * CY)
    layer_index = remainder // CY
    first_cell = jnp.where(side_index == 0, layer_index, CX - 1 - layer_index)
    across_rows = component * CX * CY + first_cell * CY + remainder % CY
    component = along_picks // (2 * CX)
    remainder = along_picks % (2 * CX)
    layer_index = remainder // CX
    second_cell = jnp.where(side_index == 0, layer_index, CY - 1 - layer_index)
    along_rows = component * CX * CY + remainder % CX * CY + second_cell
    all_rows = jnp.concatenate([across_rows, along_rows], axis=1)
    return all_rows.reshape(NX // CX, NY // CY, 4, OV).astype(jnp.int32)


def shard_levels(key, extent, cuts, smallest, high):
    level, own = 1.0, jax.random.fold_in(key, 6)
    for axis_at, blocks in cuts:
        heights = jnp.exp(jax.random.uniform(jax.random.fold_in(own, axis_at), (blocks,), jnp.float32, smallest / len(cuts), high / len(cuts)))
        level = level * jnp.repeat(heights, extent[axis_at] // blocks).reshape([-1 if axis == axis_at else 1 for axis in range(len(extent))])
    return level


def gaussian(own_key, extent, scale, bound, shards=(), kind=jnp.bfloat16):
    values = jax.random.normal(own_key, extent, jnp.float32) * scale
    if len(shards) > 0:
        values = shard_levels(own_key, extent, shards, -0.22, 0.18) * values
    return jnp.clip(values, min=-bound, max=bound).astype(kind)


def setup_inputs(seed: int = 0) -> dict:
    key_of = jax.random.split(jax.random.key(seed), 8)
    return {
        "residual": gaussian(key_of[0], (3, NX, NY, NV), 1.0, 6.0, ((1, 8), (2, 4)), jnp.float32),
        "stiffness": jnp.clip(jnp.exp(math.log(2.0) - 1.3862944 * jax.random.uniform(key_of[1], (NX, NY), jnp.float32) ** shard_levels(key_of[1], (NX, NY), ((0, 8), (1, 4)), -0.2, 0.2)), 0.5, 2.0),
        "local_inverse": draw_local_inverse(jax.random.fold_in(key_of[7], 71), 0),
        "coarse_basis": gaussian(key_of[3], (N_GX, N_GY, K, M), 0.08, 0.5, ((0, 8), (1, 4))),
        "coarse_rows": draw_coarse_rows(jax.random.fold_in(key_of[7], 71), 0),
        "send_rows": draw_send_rows(jax.random.fold_in(key_of[7], 71), 0),
        "partition_map": draw_partition_map(jax.random.fold_in(key_of[7], 71), 0),
    }


def from_lower(blocks, axis):
    edge = jnp.zeros_like(lax.slice_in_dim(blocks, 0, 1, axis=axis))
    return jnp.concatenate([edge, lax.slice_in_dim(blocks, 0, blocks.shape[axis] - 1, axis=axis)], axis=axis)


def from_upper(blocks, axis):
    edge = jnp.zeros_like(lax.slice_in_dim(blocks, 0, 1, axis=axis))
    return jnp.concatenate([lax.slice_in_dim(blocks, 1, blocks.shape[axis], axis=axis), edge], axis=axis)


def pick_rows(matrix, picks):
    return jnp.take(matrix, picks, axis=0)


def project_down(group):
    return jnp.dot(group[0], group[1], preferred_element_type=jnp.float32)


def apply_local(group):
    local_part = jnp.dot(group[0], group[1], preferred_element_type=jnp.float32)
    return local_part + jnp.dot(group[2].T, group[3], preferred_element_type=jnp.float32)


def add_back(update, picks, incoming):
    update = update.at[picks[0]].add(incoming[0])
    update = update.at[picks[1]].add(incoming[1])
    update = update.at[picks[2]].add(incoming[2])
    return update.at[picks[3]].add(incoming[3])


def operate(values, stiffness):
    padded = jnp.pad(values, ((0, 0), (1, 1), (1, 1), (0, 0)))
    beside = padded[:, 2:, 1:-1] + padded[:, :-2, 1:-1] + padded[:, 1:-1, 2:] + padded[:, 1:-1, :-2]
    return (4.0 + stiffness[None, :, :, None]) * values - beside


def correct(values, local_inverse, coarse_basis, coarse_rows, send_rows, partition_map):
    grid_rows = N_GX
    grid_cols = N_GY
    device_count = grid_rows * grid_cols
    own_count = 3 * CX * CY
    own_rows = values.reshape(3, grid_rows, CX, grid_cols, CY, NV).transpose(1, 3, 0, 2, 4, 5)
    own_rows = own_rows.reshape(grid_rows, grid_cols, own_count, NV)
    outgoing = jax.vmap(jax.vmap(pick_rows))(own_rows, send_rows)
    subdomain = jnp.concatenate([own_rows, from_lower(outgoing[:, :, 1], 0), from_upper(outgoing[:, :, 0], 0),
                                 from_lower(outgoing[:, :, 3], 1), from_upper(outgoing[:, :, 2], 1)], axis=2)
    subdomain = subdomain.astype(jnp.bfloat16)
    flat_sub = subdomain.reshape(device_count, M, NV)
    flat_inverse = local_inverse.reshape(device_count, M, M)
    flat_basis = coarse_basis.reshape(device_count, K, M)
    coarse_in = lax.map(project_down, (flat_basis, flat_sub)).astype(jnp.bfloat16)
    whole_matrix = coarse_rows.reshape(KD, device_count, K)[:, partition_map, :].reshape(KD, KD)
    coarse_out = jnp.dot(whole_matrix, coarse_in.reshape(KD, NV), preferred_element_type=jnp.float32)
    coarse_out = coarse_out.astype(jnp.bfloat16).reshape(device_count, K, NV)
    patch = lax.map(apply_local, (flat_inverse, flat_sub, flat_basis, coarse_out)).reshape(grid_rows, grid_cols, M, NV)
    own_patch = patch[:, :, :own_count]
    back_zero = from_lower(patch[:, :, own_count + OV:own_count + 2 * OV], 0)
    back_one = from_upper(patch[:, :, own_count:own_count + OV], 0)
    back_two = from_lower(patch[:, :, own_count + 3 * OV:], 1)
    back_three = from_upper(patch[:, :, own_count + 2 * OV:own_count + 3 * OV], 1)
    incoming = jnp.stack([back_zero, back_one, back_two, back_three], axis=2)
    update = jax.vmap(jax.vmap(add_back))(own_patch, send_rows, incoming)
    update = update.reshape(grid_rows, grid_cols, 3, CX, CY, NV).transpose(2, 0, 3, 1, 4, 5)
    return update.reshape(3, NX, NY, NV)


def reference(residual, stiffness, local_inverse, coarse_basis, coarse_rows, send_rows, partition_map):
    first_pass = correct(residual, local_inverse, coarse_basis, coarse_rows, send_rows, partition_map)
    middle = residual - operate(first_pass, stiffness)
    second_pass = correct(middle, local_inverse, coarse_basis, coarse_rows, send_rows, partition_map)
    solution = first_pass + second_pass
    return solution, residual - operate(solution, stiffness)
```

```python
import functools

import jax
import jax.numpy as jnp
from jax import lax
from jax.experimental import pallas as pl
from jax.experimental.pallas import tpu as pltpu
from jax.sharding import PartitionSpec as P

MESH = pl.DeviceIdType.MESH
F32 = jnp.float32
BF16 = jnp.bfloat16
HIGH = lax.Precision.HIGHEST


def dot(x, y, **kw):
    return jnp.dot(x, y, preferred_element_type=F32, **kw)


def tdot(x, y):
    return lax.dot_general(x, y, (((0,), (0,)), ((), ())), preferred_element_type=F32)


def fiota(shape, axis):
    return lax.broadcasted_iota(jnp.int32, shape, axis).astype(F32)


def fdiv(x, n):
    return jnp.floor((x + 0.5) * (1.0 / n))


def kernel(
    gx, gy, dims,
    res_hbm, stiff_ref, inv_hbm, basis_ref, crows_ref, lists_ref, pmap_ref,
    sol_ref, fin_ref,
    res_v, inv_v, sub, sel, selt, outs, backs, backr, hs, hr, allbuf,
    sext, bsend, brecv, bext, diag, m_lo, m_hi, xs, mid,
    lsem, nsem_s, nsem_r, csem_s, csem_r, g1s, g1r, g2s, g2r,
):
    comps, cx, cy, nv = dims
    own = comps * cx * cy
    layer = cx * cy
    ov = lists_ref.shape[1]
    kw, kd = crows_ref.shape
    a = lax.axis_index("gx")
    b = lax.axis_index("gy")

    load_res = pltpu.make_async_copy(res_hbm, res_v, lsem.at[0])
    load_inv = pltpu.make_async_copy(inv_hbm, inv_v, lsem.at[1])
    load_res.start()
    load_inv.start()

    barrier = pltpu.get_barrier_semaphore()
    for o in range(1, gx):
        pl.semaphore_signal(barrier, inc=1, device_id=(lax.rem(a + o, gx), b), device_id_type=MESH)
    for o in range(1, gy):
        pl.semaphore_signal(barrier, inc=1, device_id=(a, lax.rem(b + o, gy)), device_id_type=MESH)

    up = [(a + 1, b), (a - 1, b), (a, b + 1), (a, b - 1)]
    has_up = [a < gx - 1, a > 0, b < gy - 1, b > 0]
    down = [up[p ^ 1] for p in range(4)]
    has_down = [has_up[p ^ 1] for p in range(4)]
    finish = []

    def send(copies, conds, wait):
        for p in range(4):
            @pl.when(conds[p])
            def _(p=p):
                for c in copies(p):
                    getattr(c, wait)()

    def trade(copies, forward):
        to, fro = (has_up, has_down) if forward else (has_down, has_up)
        send(copies, to, "start")
        finish.append(lambda: send(copies, to, "wait_send"))
        return lambda: send(copies, fro, "wait_recv")

    def remote(src, dst, s, r, dev):
        return pltpu.make_async_remote_copy(
            src_ref=src, dst_ref=dst, send_sem=s, recv_sem=r, device_id=dev, device_id_type=MESH
        )

    rows = fiota((own, ov), 0)
    lists = lists_ref[...].astype(F32)
    for h in range(2):
        two = [jnp.where(rows == lists[p ^ 1 : (p ^ 1) + 1], 1.0, 0.0) for p in (2 * h, 2 * h + 1)]
        both = jnp.concatenate(two, axis=1)
        sel[:, 2 * ov * h : 2 * ov * (h + 1)] = both.astype(BF16)
        selt[2 * ov * h : 2 * ov * (h + 1), :] = both.T.astype(BF16)

    for p in range(4):
        at = own + p * ov

        @pl.when(jnp.logical_not(has_down[p]))
        def _(p=p, at=at):
            for t in range(2):
                sub[t, at : at + ov, :] = jnp.zeros((ov, nv), BF16)
                hr[t, p] = jnp.zeros(hr.shape[2:], F32)

        @pl.when(jnp.logical_not(has_up[p]))
        def _(p=p):
            for t in range(2):
                backr[t, p * ov : (p + 1) * ov, :] = jnp.zeros((ov, nv), BF16)
            sext[(p + 1) * kw : (p + 2) * kw, :] = jnp.zeros((kw, kd), F32)
            brecv[p * kw : (p + 1) * kw, :] = jnp.zeros((kw, 4 * ov), F32)

    load_res.wait()

    def gather(t, src):
        value = src[...].astype(BF16)
        sub[t, :own, :] = value
        outs[t] = dot(selt[...], value).astype(BF16)

    gather(0, res_v)
    pl.semaphore_wait(barrier, gx + gy - 2)

    def start_margins(t):
        return trade(
            lambda p: [remote(outs.at[t, pl.ds(p * ov, ov)], sub.at[t, pl.ds(own + p * ov, ov)],
                              nsem_s.at[t, 0, p], nsem_r.at[t, 0, p], up[p])],
            True,
        )

    wait_margins = start_margins(0)

    wide = min(kd, 256)
    n = gx * gy
    pmf = jnp.broadcast_to(pmap_ref[...].astype(F32), (8, n))

    def order(c, _):
        q = fiota((1, wide), 1) + (c * wide).astype(F32)
        slot = fdiv(q, kw)
        slab = fdiv(slot, gx)
        dev = (slot - slab * gx) * gy + slab
        pick = jnp.where(fiota((n, wide), 0) == dev, 1.0, 0.0)
        place = dot(pmf, pick, precision=HIGH)[0:1] * kw + (q - slot * kw)
        perm = jnp.where(fiota((kd, wide), 0) == place, 1.0, 0.0).astype(BF16)
        sext[0:kw, pl.ds(pl.multiple_of(c * wide, wide), wide)] = dot(crows_ref[...], perm)
        return 0

    lax.fori_loop(jnp.int32(0), jnp.int32(kd // wide), order, 0)
    bsend[...] = basis_ref[:, own:].astype(F32)
    wait_coarse = trade(
        lambda p: [
            remote(sext.at[pl.ds(0, kw)], sext.at[pl.ds((p + 1) * kw, kw)], csem_s.at[0, p], csem_r.at[0, p], down[p]),
            remote(bsend, brecv.at[pl.ds(p * kw, kw)], csem_s.at[1, p], csem_r.at[1, p], down[p]),
        ],
        False,
    )

    r1 = fiota((layer, cy), 0)
    first = fdiv(r1, cy)
    mine = jnp.where(fiota((layer, cx), 1) == fdiv(fiota((layer, cx), 0), cy), 1.0, 0.0)
    spread = dot(mine, stiff_ref[...], precision=HIGH)
    spread = jnp.where(fiota((layer, cy), 1) == r1 - first * cy, spread, 0.0)
    diag[...] = jnp.broadcast_to(4.0 + jnp.sum(spread, axis=1, keepdims=True), (layer, nv))
    rr = fiota((layer, nv), 0)
    second = rr - fdiv(rr, cy) * cy
    m_lo[...] = jnp.where(second == 0.0, 0.0, 1.0)
    m_hi[...] = jnp.where(second == cy - 1.0, 0.0, 1.0)

    def correct(t, src, dst, wait_margins):
        if t == 0:
            load_inv.wait()
        part = dot(inv_v[:, :own], sub[t, :own, :])
        cpart = dot(basis_ref[:, :own], sub[t, :own, :])
        wait_margins()
        edge = sub[t, own:, :]
        cin = cpart + dot(basis_ref[:, own:], edge)
        allbuf[t, b, a] = cin.astype(BF16)

        def stage1(o, dev, slot):
            ref = allbuf.at[t, b, slot]
            return remote(ref, ref, g1s.at[t, o], g1r.at[t, o], (dev, b))

        def stage2(o, dev, slot):
            ref = allbuf.at[t, slot]
            return remote(ref, ref, g2s.at[t, o], g2r.at[t, o], (a, dev))

        for o in range(1, gx):
            stage1(o, lax.rem(a + o, gx), a).start()
        patch = part + dot(inv_v[:, own:], edge)
        backs[t] = patch[own:].astype(BF16)
        wait_back = trade(
            lambda p: [remote(backs.at[t, pl.ds(p * ov, ov)], backr.at[t, pl.ds(p * ov, ov)],
                              nsem_s.at[t, 1, p], nsem_r.at[t, 1, p], down[p])],
            False,
        )
        xs[...] = patch[:own]
        for o in range(1, gx):
            stage1(o, lax.rem(a + o, gx), lax.rem(a + (gx - o), gx)).wait_recv()
        for o in range(1, gy):
            stage2(o, lax.rem(b + o, gy), b).start()
        if t == 0:
            wait_coarse()
            rb = fdiv(fiota((4 * kw, 4 * ov), 0), kw)
            cb = fdiv(fiota((4 * kw, 4 * ov), 1), ov)
            margins = jnp.where(rb == cb, brecv[...], 0.0).astype(BF16)
            below = dot(margins, selt[...])
            ext = jnp.concatenate([basis_ref[:, :own].astype(F32), below], axis=0)
            bext[...] = ext.T.astype(BF16)
        wait_back()
        xs[...] += dot(sel[...], backr[t])
        for o in range(1, gy):
            stage2(o, lax.rem(b + o, gy), lax.rem(b + (gy - o), gy)).wait_recv()
        gathered = allbuf[t].astype(F32).reshape(kd, nv).astype(BF16)
        cout = dot(sext[...].astype(BF16), gathered).astype(BF16)
        xs[...] += dot(bext[...], cout)

        def done():
            for o in range(1, gx):
                stage1(o, lax.rem(a + o, gx), a).wait_send()
            for o in range(1, gy):
                stage2(o, lax.rem(b + o, gy), b).wait_send()

        finish.append(done)

        for c in range(comps):
            base = c * layer
            hs[t, 0, c * cy : (c + 1) * cy, :] = xs[base + layer - cy : base + layer, :]
            hs[t, 1, c * cy : (c + 1) * cy, :] = xs[base : base + cy, :]
        hs[t, 2, : comps * cx, :] = xs[pl.ds(cy - 1, comps * cx, stride=cy), :]
        hs[t, 3, : comps * cx, :] = xs[pl.ds(0, comps * cx, stride=cy), :]
        wait_halo = trade(
            lambda p: [remote(hs.at[t, p], hr.at[t, p], nsem_s.at[t, 2, p], nsem_r.at[t, 2, p], up[p])],
            True,
        )
        zero = jnp.zeros((cy, nv), F32)
        for c in range(comps):
            at = pl.ds(c * layer, layer)
            x = xs[at, :]
            beside = jnp.concatenate([zero, x[:-cy]], axis=0) + jnp.concatenate([x[cy:], zero], axis=0)
            beside += pltpu.roll(x, 1, 0) * m_lo[...] + pltpu.roll(x, layer - 1, 0) * m_hi[...]
            dst[at, :] = src[at, :] - (diag[...] * x - beside)
        return wait_halo

    def finish_halo(t, dst, wait_halo):
        wait_halo()
        for c in range(comps):
            base = c * layer
            dst[base : base + cy, :] += hr[t, 0, c * cy : (c + 1) * cy, :]
            dst[base + layer - cy : base + layer, :] += hr[t, 1, c * cy : (c + 1) * cy, :]
        low = pl.ds(0, comps * cx, stride=cy)
        high = pl.ds(cy - 1, comps * cx, stride=cy)
        dst[low, :] = dst[low, :] + hr[t, 2, : comps * cx, :]
        dst[high, :] = dst[high, :] + hr[t, 3, : comps * cx, :]

    wait_halo = correct(0, res_v, mid, wait_margins)
    sol_ref[...] = xs[...]
    finish_halo(0, mid, wait_halo)
    gather(1, mid)
    wait_halo = correct(1, mid, fin_ref, start_margins(1))
    sol_ref[...] += xs[...]
    finish_halo(1, fin_ref, wait_halo)
    for end in finish:
        end()


def solution(mesh):
    gx, gy = mesh.shape["gx"], mesh.shape["gy"]

    def per_device(residual, stiffness, local_inverse, coarse_basis, coarse_rows, send_rows, partition_map):
        comps, cx, cy, nv = residual.shape
        own, layer = comps * cx * cy, cx * cy
        m = local_inverse.shape[-1]
        ov = send_rows.shape[-1]
        kw, kd = coarse_rows.shape[-2:]
        halo = comps * max(cx, cy)
        vm = pl.BlockSpec(memory_space=pltpu.VMEM)
        anywhere = pl.BlockSpec(memory_space=pl.ANY)
        dma = pltpu.SemaphoreType.DMA
        out = pl.pallas_call(
            functools.partial(kernel, gx, gy, (comps, cx, cy, nv)),
            out_shape=[jax.ShapeDtypeStruct((own, nv), F32)] * 2,
            in_specs=[anywhere, vm, anywhere, vm, vm, vm, vm],
            out_specs=[vm, vm],
            scratch_shapes=[
                pltpu.VMEM((own, nv), F32),
                pltpu.VMEM((m, m), BF16),
                pltpu.VMEM((2, m, nv), BF16),
                pltpu.VMEM((own, 4 * ov), BF16),
                pltpu.VMEM((4 * ov, own), BF16),
                pltpu.VMEM((2, 4 * ov, nv), BF16),
                pltpu.VMEM((2, 4 * ov, nv), BF16),
                pltpu.VMEM((2, 4 * ov, nv), BF16),
                pltpu.VMEM((2, 4, halo, nv), F32),
                pltpu.VMEM((2, 4, halo, nv), F32),
                pltpu.VMEM((2, gy, gx, kw, nv), BF16),
                pltpu.VMEM((5 * kw, kd), F32),
                pltpu.VMEM((kw, m - own), F32),
                pltpu.VMEM((4 * kw, m - own), F32),
                pltpu.VMEM((own, 5 * kw), BF16),
                pltpu.VMEM((layer, nv), F32),
                pltpu.VMEM((layer, nv), F32),
                pltpu.VMEM((layer, nv), F32),
                pltpu.VMEM((own, nv), F32),
                pltpu.VMEM((own, nv), F32),
                dma((2,)),
                dma((2, 3, 4)),
                dma((2, 3, 4)),
                dma((2, 4)),
                dma((2, 4)),
                dma((2, gx)),
                dma((2, gx)),
                dma((2, gy)),
                dma((2, gy)),
            ],
            compiler_params=pltpu.CompilerParams(collective_id=0, has_side_effects=True),
        )(
            residual.reshape(own, nv),
            stiffness,
            local_inverse[0, 0],
            coarse_basis[0, 0],
            coarse_rows[0, 0],
            send_rows[0, 0],
            partition_map.reshape(1, -1),
        )
        return tuple(o.reshape(residual.shape) for o in out)

    placed = (
        P(None, "gx", "gy", None),
        P("gx", "gy"),
        P("gx", "gy", None, None),
        P("gx", "gy", None, None),
        P("gx", "gy", None, None),
        P("gx", "gy", None, None),
        P(),
    )
    return jax.shard_map(
        per_device,
        mesh=mesh,
        in_specs=placed,
        out_specs=(P(None, "gx", "gy", None), P(None, "gx", "gy", None)),
        check_vma=False,
    )
```

```python
import functools

import jax
import jax.numpy as jnp
from jax import lax
from jax.experimental import pallas as pl
from jax.experimental.pallas import tpu as pltpu
from jax.sharding import PartitionSpec as P

MESH = pl.DeviceIdType.MESH
F32 = jnp.float32
BF16 = jnp.bfloat16
HIGH = lax.Precision.HIGHEST


def dot(x, y, **kw):
    return jnp.dot(x, y, preferred_element_type=F32, **kw)


def tdot(x, y):
    return lax.dot_general(x, y, (((0,), (0,)), ((), ())), preferred_element_type=F32)


def fiota(shape, axis):
    return lax.broadcasted_iota(jnp.int32, shape, axis).astype(F32)


def fdiv(x, n):
    return jnp.floor((x + 0.5) * (1.0 / n))


def kernel(
    gx, gy, dims,
    res_hbm, stiff_ref, inv_hbm, basis_ref, crows_ref, lists_ref, pmap_ref,
    sol_ref, fin_ref,
    res_v, inv_v, sub, sel, selt, outs, backs, backr, hs, hr, allbuf,
    sext, bsend, brecv, bextf, cmat, csend, diag, m_lo, m_hi, xs, mid,
    lsem, nsem_s, nsem_r, csem_s, csem_r, g1s, g1r, g2s, g2r,
):
    comps, cx, cy, nv = dims
    halo = hr.shape[2]
    hrows = (comps * cy, comps * cy, comps * cx, comps * cx)
    own = comps * cx * cy
    layer = cx * cy
    ov = lists_ref.shape[1]
    kw, kd = crows_ref.shape
    a = lax.axis_index("gx")
    b = lax.axis_index("gy")

    load_res = pltpu.make_async_copy(res_hbm, res_v, lsem.at[0])
    load_inv = pltpu.make_async_copy(inv_hbm, inv_v, lsem.at[1])
    load_res.start()
    load_inv.start()

    barrier = pltpu.get_barrier_semaphore()
    for o in range(1, gx):
        pl.semaphore_signal(barrier, inc=1, device_id=(lax.rem(a + o, gx), b), device_id_type=MESH)
    for o in range(1, gy):
        pl.semaphore_signal(barrier, inc=1, device_id=(a, lax.rem(b + o, gy)), device_id_type=MESH)

    up = [(a + 1, b), (a - 1, b), (a, b + 1), (a, b - 1)]
    has_up = [a < gx - 1, a > 0, b < gy - 1, b > 0]
    down = [up[p ^ 1] for p in range(4)]
    has_down = [has_up[p ^ 1] for p in range(4)]
    finish = []

    def send(copies, conds, wait):
        for p in range(4):
            @pl.when(conds[p])
            def _(p=p):
                for c in copies(p):
                    getattr(c, wait)()

    def trade(copies, forward):
        to, fro = (has_up, has_down) if forward else (has_down, has_up)
        send(copies, to, "start")
        finish.append(lambda: send(copies, to, "wait_send"))
        return lambda: send(copies, fro, "wait_recv")

    def remote(src, dst, s, r, dev):
        return pltpu.make_async_remote_copy(
            src_ref=src, dst_ref=dst, send_sem=s, recv_sem=r, device_id=dev, device_id_type=MESH
        )

    rows = fiota((own, ov), 0)
    lists = lists_ref[...].astype(F32)
    for h in range(2):
        two = [jnp.where(rows == lists[p ^ 1 : (p ^ 1) + 1], 1.0, 0.0) for p in (2 * h, 2 * h + 1)]
        both = jnp.concatenate(two, axis=1)
        sel[:, 2 * ov * h : 2 * ov * (h + 1)] = both.astype(BF16)
        selt[2 * ov * h : 2 * ov * (h + 1), :] = both.T.astype(BF16)

    for p in range(4):
        at = own + p * ov

        @pl.when(jnp.logical_not(has_down[p]))
        def _(p=p, at=at):
            for t in range(2):
                sub[t, at : at + ov, :] = jnp.zeros((ov, nv), BF16)
                hr[t, p] = jnp.zeros(hr.shape[2:], BF16)

        @pl.when(jnp.logical_not(has_up[p]))
        def _(p=p):
            for t in range(2):
                backr[t, p * ov : (p + 1) * ov, :] = jnp.zeros((ov, nv), BF16)
            sext[(p + 1) * kw : (p + 2) * kw, :] = jnp.zeros((kw, kd), F32)
            brecv[p * kw : (p + 1) * kw, :] = jnp.zeros((kw, 4 * ov), F32)

        @pl.when(jnp.logical_not(has_down[p]))
        def _(p=p):
            cmat[own + p * halo : own + (p + 1) * halo, :] = jnp.zeros((halo, kd), BF16)

    sext[5 * kw :, :] = jnp.zeros((sext.shape[0] - 5 * kw, kd), F32)

    load_res.wait()

    def gather(t, src):
        value = src[...].astype(BF16)
        sub[t, :own, :] = value
        outs[t] = dot(selt[...], value).astype(BF16)

    gather(0, res_v)
    pl.semaphore_wait(barrier, gx + gy - 2)

    def start_margins(t):
        return trade(
            lambda p: [remote(outs.at[t, pl.ds(p * ov, ov)], sub.at[t, pl.ds(own + p * ov, ov)],
                              nsem_s.at[t, 0, p], nsem_r.at[t, 0, p], up[p])],
            True,
        )

    wait_margins = start_margins(0)

    wide = min(kd, 256)
    n = gx * gy
    pmf = jnp.broadcast_to(pmap_ref[...].astype(F32), (8, n))

    def order(c, _):
        q = fiota((1, wide), 1) + (c * wide).astype(F32)
        slot = fdiv(q, kw)
        slab = fdiv(slot, gx)
        dev = (slot - slab * gx) * gy + slab
        pick = jnp.where(fiota((n, wide), 0) == dev, 1.0, 0.0)
        place = dot(pmf, pick, precision=HIGH)[0:1] * kw + (q - slot * kw)
        perm = jnp.where(fiota((kd, wide), 0) == place, 1.0, 0.0).astype(BF16)
        sext[0:kw, pl.ds(pl.multiple_of(c * wide, wide), wide)] = dot(crows_ref[...], perm)
        return 0

    lax.fori_loop(jnp.int32(0), jnp.int32(kd // wide), order, 0)
    bsend[...] = basis_ref[:, own:].astype(F32)
    wait_coarse = trade(
        lambda p: [
            remote(sext.at[pl.ds(0, kw)], sext.at[pl.ds((p + 1) * kw, kw)], csem_s.at[0, p], csem_r.at[0, p], down[p]),
            remote(bsend, brecv.at[pl.ds(p * kw, kw)], csem_s.at[1, p], csem_r.at[1, p], down[p]),
        ],
        False,
    )

    r1 = fiota((layer, cy), 0)
    first = fdiv(r1, cy)
    mine = jnp.where(fiota((layer, cx), 1) == fdiv(fiota((layer, cx), 0), cy), 1.0, 0.0)
    spread = dot(mine, stiff_ref[...], precision=HIGH)
    spread = jnp.where(fiota((layer, cy), 1) == r1 - first * cy, spread, 0.0)
    diag[...] = jnp.broadcast_to(4.0 + jnp.sum(spread, axis=1, keepdims=True), (layer, nv))
    rr = fiota((layer, nv), 0)
    second = rr - fdiv(rr, cy) * cy
    m_lo[...] = jnp.where(second == 0.0, 0.0, 1.0)
    m_hi[...] = jnp.where(second == cy - 1.0, 0.0, 1.0)

    def layer_rows(ref, p):
        if p >= 2:
            return ref[pl.ds((cy - 1) * (3 - p), comps * cx, stride=cy), :]
        skip = (layer - cy) * (1 - p)
        return jnp.concatenate([ref[c * layer + skip : c * layer + skip + cy, :] for c in range(comps)], axis=0)

    wait_edges = []

    def correct(t, src, dst, wait_margins):
        if t == 0:
            load_inv.wait()
        part = dot(inv_v[:, :own], sub[t, :own, :])
        cpart = dot(basis_ref[:, :own], sub[t, :own, :])
        wait_margins()
        edge = sub[t, own:, :]
        cin = cpart + dot(basis_ref[:, own:], edge)
        allbuf[t, b, a] = cin.astype(BF16)

        def stage1(o, dev, slot):
            ref = allbuf.at[t, b, slot]
            return remote(ref, ref, g1s.at[t, o], g1r.at[t, o], (dev, b))

        def stage2(o, dev, slot):
            ref = allbuf.at[t, slot]
            return remote(ref, ref, g2s.at[t, o], g2r.at[t, o], (a, dev))

        for o in range(1, gx):
            stage1(o, lax.rem(a + o, gx), a).start()
        patch = part + dot(inv_v[:, own:], edge)
        backs[t] = patch[own:].astype(BF16)
        wait_back = trade(
            lambda p: [remote(backs.at[t, pl.ds(p * ov, ov)], backr.at[t, pl.ds(p * ov, ov)],
                              nsem_s.at[t, 1, p], nsem_r.at[t, 1, p], down[p])],
            False,
        )
        xs[...] = patch[:own]
        if t == 0:
            wait_coarse()
            rb = fdiv(fiota((4 * kw, 4 * ov), 0), kw)
            cb = fdiv(fiota((4 * kw, 4 * ov), 1), ov)
            margins = jnp.where(rb == cb, brecv[...], 0.0).astype(BF16)
            below = dot(margins, selt[...])
            rest = jnp.zeros((sext.shape[0] - 5 * kw, own), F32)
            ext = jnp.concatenate([basis_ref[:, :own].astype(F32), below, rest], axis=0)
            bextf[...] = ext.T
            edges = jnp.concatenate([layer_rows(bextf, p) for p in range(4)], axis=0).astype(BF16)

            def build(c, _):
                at = pl.ds(pl.multiple_of(c * wide, wide), wide)
                part_s = sext[:, at].astype(BF16)
                csend[:, at] = dot(edges, part_s).astype(BF16)
                cmat[:own, at] = dot(bextf[...].astype(BF16), part_s).astype(BF16)
                return 0

            lax.fori_loop(jnp.int32(0), jnp.int32(kd // wide), build, 0)
            wait_edges.append(trade(
                lambda p: [remote(csend.at[pl.ds(p * halo, halo)], cmat.at[pl.ds(own + p * halo, halo)],
                                  csem_s.at[2, p], csem_r.at[2, p], up[p])],
                True,
            ))
        for o in range(1, gx):
            stage1(o, lax.rem(a + o, gx), lax.rem(a + (gx - o), gx)).wait_recv()
        for o in range(1, gy):
            stage2(o, lax.rem(b + o, gy), b).start()
        wait_back()
        xs[...] += dot(sel[...], backr[t])

        for p in range(4):
            hs[t, p, : hrows[p], :] = layer_rows(xs, p).astype(hs.dtype)
        wait_halo = trade(
            lambda p: [remote(hs.at[t, p], hr.at[t, p], nsem_s.at[t, 2, p], nsem_r.at[t, 2, p], up[p])],
            True,
        )
        if t == 0:
            wait_edges[0]()
        for o in range(1, gy):
            stage2(o, lax.rem(b + o, gy), lax.rem(b + (gy - o), gy)).wait_recv()
        gathered = allbuf[t].astype(F32).reshape(kd, nv).astype(BF16)
        coarse = dot(cmat[...], gathered)
        xs[...] += coarse[:own]
        far = coarse[own:]

        def done():
            for o in range(1, gx):
                stage1(o, lax.rem(a + o, gx), a).wait_send()
            for o in range(1, gy):
                stage2(o, lax.rem(b + o, gy), b).wait_send()

        finish.append(done)

        zero = jnp.zeros((cy, nv), F32)
        for c in range(comps):
            at = pl.ds(c * layer, layer)
            x = xs[at, :]
            beside = jnp.concatenate([zero, x[:-cy]], axis=0) + jnp.concatenate([x[cy:], zero], axis=0)
            beside += pltpu.roll(x, 1, 0) * m_lo[...] + pltpu.roll(x, layer - 1, 0) * m_hi[...]
            dst[at, :] = src[at, :] - (diag[...] * x - beside)
        wait_halo()
        around = [hr[t, p, : hrows[p], :].astype(F32) + far[p * halo : p * halo + hrows[p]] for p in range(4)]
        for c in range(comps):
            base = c * layer
            dst[base : base + cy, :] += around[0][c * cy : (c + 1) * cy]
            dst[base + layer - cy : base + layer, :] += around[1][c * cy : (c + 1) * cy]
        low = pl.ds(0, comps * cx, stride=cy)
        high = pl.ds(cy - 1, comps * cx, stride=cy)
        dst[low, :] = dst[low, :] + around[2]
        dst[high, :] = dst[high, :] + around[3]

    correct(0, res_v, mid, wait_margins)
    gather(1, mid)
    wait_margins = start_margins(1)
    sol_ref[...] = xs[...]
    correct(1, mid, fin_ref, wait_margins)
    sol_ref[...] += xs[...]
    for end in finish:
        end()


def solution(mesh):
    gx, gy = mesh.shape["gx"], mesh.shape["gy"]

    def per_device(residual, stiffness, local_inverse, coarse_basis, coarse_rows, send_rows, partition_map):
        comps, cx, cy, nv = residual.shape
        own, layer = comps * cx * cy, cx * cy
        m = local_inverse.shape[-1]
        ov = send_rows.shape[-1]
        kw, kd = coarse_rows.shape[-2:]
        halo = comps * max(cx, cy)
        lanes = -(-5 * kw // 128) * 128
        vm = pl.BlockSpec(memory_space=pltpu.VMEM)
        anywhere = pl.BlockSpec(memory_space=pl.ANY)
        dma = pltpu.SemaphoreType.DMA
        out = pl.pallas_call(
            functools.partial(kernel, gx, gy, (comps, cx, cy, nv)),
            out_shape=[jax.ShapeDtypeStruct((own, nv), F32)] * 2,
            in_specs=[anywhere, vm, anywhere, vm, vm, vm, vm],
            out_specs=[vm, vm],
            scratch_shapes=[
                pltpu.VMEM((own, nv), F32),
                pltpu.VMEM((m, m), BF16),
                pltpu.VMEM((2, m, nv), BF16),
                pltpu.VMEM((own, 4 * ov), BF16),
                pltpu.VMEM((4 * ov, own), BF16),
                pltpu.VMEM((2, 4 * ov, nv), BF16),
                pltpu.VMEM((2, 4 * ov, nv), BF16),
                pltpu.VMEM((2, 4 * ov, nv), BF16),
                pltpu.VMEM((2, 4, halo, nv), BF16),
                pltpu.VMEM((2, 4, halo, nv), BF16),
                pltpu.VMEM((2, gy, gx, kw, nv), BF16),
                pltpu.VMEM((lanes, kd), F32),
                pltpu.VMEM((kw, m - own), F32),
                pltpu.VMEM((4 * kw, m - own), F32),
                pltpu.VMEM((own, lanes), F32),
                pltpu.VMEM((own + 4 * halo, kd), BF16),
                pltpu.VMEM((4 * halo, kd), BF16),
                pltpu.VMEM((layer, nv), F32),
                pltpu.VMEM((layer, nv), F32),
                pltpu.VMEM((layer, nv), F32),
                pltpu.VMEM((own, nv), F32),
                pltpu.VMEM((own, nv), F32),
                dma((2,)),
                dma((2, 3, 4)),
                dma((2, 3, 4)),
                dma((3, 4)),
                dma((3, 4)),
                dma((2, gx)),
                dma((2, gx)),
                dma((2, gy)),
                dma((2, gy)),
            ],
            compiler_params=pltpu.CompilerParams(collective_id=0, has_side_effects=True),
        )(
            residual.reshape(own, nv),
            stiffness,
            local_inverse[0, 0],
            coarse_basis[0, 0],
            coarse_rows[0, 0],
            send_rows[0, 0],
            partition_map.reshape(1, -1),
        )
        return tuple(o.reshape(residual.shape) for o in out)

    placed = (
        P(None, "gx", "gy", None),
        P("gx", "gy"),
        P("gx", "gy", None, None),
        P("gx", "gy", None, None),
        P("gx", "gy", None, None),
        P("gx", "gy", None, None),
        P(),
    )
    return jax.shard_map(
        per_device,
        mesh=mesh,
        in_specs=placed,
        out_specs=(P(None, "gx", "gy", None), P(None, "gx", "gy", None)),
        check_vma=False,
    )
```

```python
import functools

import jax
import jax.numpy as jnp
from jax import lax
from jax.experimental import pallas as pl
from jax.experimental.pallas import tpu as pltpu
from jax.sharding import PartitionSpec as P

MESH = pl.DeviceIdType.MESH
F32 = jnp.float32
BF16 = jnp.bfloat16
HIGH = lax.Precision.HIGHEST


def dot(x, y, **kw):
    return jnp.dot(x, y, preferred_element_type=F32, **kw)


def tdot(x, y):
    return lax.dot_general(x, y, (((0,), (0,)), ((), ())), preferred_element_type=F32)


def fiota(shape, axis):
    return lax.broadcasted_iota(jnp.int32, shape, axis).astype(F32)


def fdiv(x, n):
    return jnp.floor((x + 0.5) * (1.0 / n))


def kernel(
    gx, gy, dims,
    res_hbm, stiff_hbm, inv_hbm, basis_hbm, crows_hbm, lists_hbm, pmap_hbm,
    sol_ref, fin_ref,
    res_v, stiff_ref, inv_v, basis_ref, crows_ref, lists_ref, pmap_ref, sub, sel, selt, outs, backs, backr, hs, hr, allbuf,
    sext, bsend, brecv, bextf, cmat, acmat, csend, diag, m_lo, m_hi, xs, mid,
    lsem, nsem_s, nsem_r, csem_s, csem_r, g1s, g1r, g2s, g2r,
):
    comps, cx, cy, nv = dims
    halo = hr.shape[2]
    hrows = (comps * cy, comps * cy, comps * cx, comps * cx)
    own = comps * cx * cy
    layer = cx * cy
    ov = lists_ref.shape[1]
    kw, kd = crows_ref.shape
    a = lax.axis_index("gx")
    b = lax.axis_index("gy")

    wanted = [
        (lists_hbm, lists_ref), (res_hbm, res_v), (pmap_hbm, pmap_ref), (crows_hbm, crows_ref),
        (basis_hbm, basis_ref), (stiff_hbm, stiff_ref), (inv_hbm, inv_v),
    ]
    loads = [pltpu.make_async_copy(x, y, lsem.at[k]) for k, (x, y) in enumerate(wanted)]
    load_lists, load_res, load_pmap, load_crows, load_basis, load_stiff, load_inv = loads
    barrier = pltpu.get_barrier_semaphore()
    for o in range(1, gx):
        pl.semaphore_signal(barrier, inc=1, device_id=(lax.rem(a + o, gx), b), device_id_type=MESH)
    for o in range(1, gy):
        pl.semaphore_signal(barrier, inc=1, device_id=(a, lax.rem(b + o, gy)), device_id_type=MESH)

    for load in loads:
        load.start()

    up = [(a + 1, b), (a - 1, b), (a, b + 1), (a, b - 1)]
    has_up = [a < gx - 1, a > 0, b < gy - 1, b > 0]
    down = [up[p ^ 1] for p in range(4)]
    has_down = [has_up[p ^ 1] for p in range(4)]
    finish = []

    def send(copies, conds, wait):
        for p in (2, 3, 0, 1):
            @pl.when(conds[p])
            def _(p=p):
                for c in copies(p):
                    getattr(c, wait)()

    def trade(copies, forward):
        to, fro = (has_up, has_down) if forward else (has_down, has_up)
        send(copies, to, "start")
        finish.append(lambda: send(copies, to, "wait_send"))
        return lambda: send(copies, fro, "wait_recv")

    def remote(src, dst, s, r, dev):
        return pltpu.make_async_remote_copy(
            src_ref=src, dst_ref=dst, send_sem=s, recv_sem=r, device_id=dev, device_id_type=MESH
        )

    load_lists.wait()
    rows = fiota((own, ov), 0)
    lists = lists_ref[...].astype(F32)
    for h in range(2):
        two = [jnp.where(rows == lists[p ^ 1 : (p ^ 1) + 1], 1.0, 0.0) for p in (2 * h, 2 * h + 1)]
        both = jnp.concatenate(two, axis=1)
        sel[:, 2 * ov * h : 2 * ov * (h + 1)] = both.astype(BF16)
        selt[2 * ov * h : 2 * ov * (h + 1), :] = both.T.astype(BF16)

    for p in range(4):
        at = own + p * ov

        @pl.when(jnp.logical_not(has_down[p]))
        def _(p=p, at=at):
            for t in range(2):
                sub[t, at : at + ov, :] = jnp.zeros((ov, nv), BF16)
                hr[t, p] = jnp.zeros(hr.shape[2:], BF16)

        @pl.when(jnp.logical_not(has_up[p]))
        def _(p=p):
            for t in range(2):
                backr[t, p * ov : (p + 1) * ov, :] = jnp.zeros((ov, nv), BF16)
            sext[(p + 1) * kw : (p + 2) * kw, :] = jnp.zeros((kw, kd), F32)
            brecv[p * kw : (p + 1) * kw, :] = jnp.zeros((kw, 4 * ov), F32)

        @pl.when(jnp.logical_not(has_down[p]))
        def _(p=p):
            cmat[own + p * halo : own + (p + 1) * halo, :] = jnp.zeros((halo, kd), BF16)

    sext[5 * kw :, :] = jnp.zeros((sext.shape[0] - 5 * kw, kd), F32)

    load_res.wait()

    def gather(t, src):
        value = src[...].astype(BF16)
        sub[t, :own, :] = value
        outs[t] = dot(selt[...], value).astype(BF16)

    gather(0, res_v)
    pl.semaphore_wait(barrier, gx + gy - 2)

    def start_margins(t):
        return trade(
            lambda p: [remote(outs.at[t, pl.ds(p * ov, ov)], sub.at[t, pl.ds(own + p * ov, ov)],
                              nsem_s.at[t, 0, p], nsem_r.at[t, 0, p], up[p])],
            True,
        )

    wait_margins = start_margins(0)

    load_pmap.wait()
    load_crows.wait()
    load_basis.wait()
    wide = min(kd, 256)
    n = gx * gy
    pmf = jnp.broadcast_to(pmap_ref[...].astype(F32), (8, n))

    def order(c, _):
        q = fiota((1, wide), 1) + (c * wide).astype(F32)
        slot = fdiv(q, kw)
        slab = fdiv(slot, gx)
        dev = (slot - slab * gx) * gy + slab
        pick = jnp.where(fiota((n, wide), 0) == dev, 1.0, 0.0)
        place = dot(pmf, pick, precision=HIGH)[0:1] * kw + (q - slot * kw)
        perm = jnp.where(fiota((kd, wide), 0) == place, 1.0, 0.0).astype(BF16)
        sext[0:kw, pl.ds(pl.multiple_of(c * wide, wide), wide)] = dot(crows_ref[...], perm)
        return 0

    lax.fori_loop(jnp.int32(0), jnp.int32(kd // wide), order, 0)
    bsend[...] = basis_ref[:, own:].astype(F32)
    wait_coarse = trade(
        lambda p: [
            remote(sext.at[pl.ds(0, kw)], sext.at[pl.ds((p + 1) * kw, kw)], csem_s.at[0, p], csem_r.at[0, p], down[p]),
            remote(bsend, brecv.at[pl.ds(p * kw, kw)], csem_s.at[1, p], csem_r.at[1, p], down[p]),
        ],
        False,
    )

    load_stiff.wait()
    r1 = fiota((layer, cy), 0)
    first = fdiv(r1, cy)
    mine = jnp.where(fiota((layer, cx), 1) == fdiv(fiota((layer, cx), 0), cy), 1.0, 0.0)
    spread = dot(mine, stiff_ref[...], precision=HIGH)
    spread = jnp.where(fiota((layer, cy), 1) == r1 - first * cy, spread, 0.0)
    diag[...] = jnp.broadcast_to(4.0 + jnp.sum(spread, axis=1, keepdims=True), (layer, nv))
    rr = fiota((layer, nv), 0)
    second = rr - fdiv(rr, cy) * cy
    m_lo[...] = jnp.where(second == 0.0, 0.0, 1.0)
    m_hi[...] = jnp.where(second == cy - 1.0, 0.0, 1.0)

    def layer_rows(ref, p):
        if p >= 2:
            return ref[pl.ds((cy - 1) * (3 - p), comps * cx, stride=cy), :]
        skip = (layer - cy) * (1 - p)
        return jnp.concatenate([ref[c * layer + skip : c * layer + skip + cy, :] for c in range(comps)], axis=0)

    def operate(x_ref, dst, src):
        zero = jnp.zeros((cy, nv), F32)
        for c in range(comps):
            at = pl.ds(c * layer, layer)
            x = x_ref[at, :]
            beside = jnp.concatenate([zero, x[:-cy]], axis=0) + jnp.concatenate([x[cy:], zero], axis=0)
            beside += pltpu.roll(x, 1, 0) * m_lo[...] + pltpu.roll(x, layer - 1, 0) * m_hi[...]
            value = beside - diag[...] * x
            dst[at, :] = value if src is None else src[at, :] + value

    def add_layers(dst, around):
        for c in range(comps):
            base = c * layer
            dst[base : base + cy, :] += around(0)[c * cy : (c + 1) * cy]
            dst[base + layer - cy : base + layer, :] += around(1)[c * cy : (c + 1) * cy]
        low = pl.ds(0, comps * cx, stride=cy)
        high = pl.ds(cy - 1, comps * cx, stride=cy)
        dst[low, :] = dst[low, :] + around(2)
        dst[high, :] = dst[high, :] + around(3)

    wait_edges = []

    def correct(t, src, dst, wait_margins):
        if t == 0:
            load_inv.wait()
        part = dot(inv_v[:, :own], sub[t, :own, :])
        cpart = dot(basis_ref[:, :own], sub[t, :own, :])
        wait_margins()
        edge = sub[t, own:, :]
        cin = cpart + dot(basis_ref[:, own:], edge)
        allbuf[t, b, a] = cin.astype(BF16)

        def stage1(o, dev, slot):
            ref = allbuf.at[t, b, slot]
            return remote(ref, ref, g1s.at[t, o], g1r.at[t, o], (dev, b))

        def stage2(o, dev, slot):
            ref = allbuf.at[t, slot]
            return remote(ref, ref, g2s.at[t, o], g2r.at[t, o], (a, dev))

        for o in range(1, gx):
            stage1(o, lax.rem(a + o, gx), a).start()
        patch = part + dot(inv_v[:, own:], edge)
        backs[t] = patch[own:].astype(BF16)
        wait_back = trade(
            lambda p: [remote(backs.at[t, pl.ds(p * ov, ov)], backr.at[t, pl.ds(p * ov, ov)],
                              nsem_s.at[t, 1, p], nsem_r.at[t, 1, p], down[p])],
            False,
        )
        xs[...] = patch[:own]
        if t == 0:
            wait_coarse()
            rb = fdiv(fiota((4 * kw, 4 * ov), 0), kw)
            cb = fdiv(fiota((4 * kw, 4 * ov), 1), ov)
            margins = jnp.where(rb == cb, brecv[...], 0.0).astype(BF16)
            below = dot(margins, selt[...])
            rest = jnp.zeros((sext.shape[0] - 5 * kw, own), F32)
            ext = jnp.concatenate([basis_ref[:, :own].astype(F32), below, rest], axis=0)
            bextf[...] = ext.T
            edges = jnp.concatenate([layer_rows(bextf, p) for p in range(4)], axis=0).astype(BF16)

            def build(c, _):
                at = pl.ds(pl.multiple_of(c * wide, wide), wide)
                part_s = sext[:, at].astype(BF16)
                csend[:, at] = dot(edges, part_s).astype(BF16)
                return 0

            lax.fori_loop(jnp.int32(0), jnp.int32(kd // wide), build, 0)
            wait_edges.append(trade(
                lambda p: [remote(csend.at[pl.ds(p * halo, halo)], cmat.at[pl.ds(own + p * halo, halo)],
                                  csem_s.at[2, p], csem_r.at[2, p], up[p])],
                True,
            ))
        for o in range(1, gx):
            stage1(o, lax.rem(a + o, gx), lax.rem(a + (gx - o), gx)).wait_recv()
        for o in range(1, gy):
            stage2(o, lax.rem(b + o, gy), b).start()
        wait_back()
        xs[...] += dot(sel[...], backr[t])

        for p in range(4):
            hs[t, p, : hrows[p], :] = layer_rows(xs, p).astype(hs.dtype)
        wait_halo = trade(
            lambda p: [remote(hs.at[t, p], hr.at[t, p], nsem_s.at[t, 2, p], nsem_r.at[t, 2, p], up[p])],
            True,
        )
        operate(xs, dst, src)
        if t == 0:
            wait_edges[0]()
            bext = bextf[...].astype(BF16)

            def fill(c, _):
                at = pl.ds(pl.multiple_of(c * nv, nv), nv)
                value = dot(bext, sext[:, at].astype(BF16))
                cmat[:own, at] = value.astype(BF16)
                sol_ref[...] = value
                operate(sol_ref, fin_ref, None)
                add_layers(fin_ref, lambda p: cmat[own + p * halo : own + p * halo + hrows[p], at].astype(F32))
                acmat[:, at] = fin_ref[...].astype(BF16)
                return 0

            lax.fori_loop(jnp.int32(0), jnp.int32(kd // nv), fill, 0)
        wait_halo()
        add_layers(dst, lambda p: hr[t, p, : hrows[p], :].astype(F32))
        for o in range(1, gy):
            stage2(o, lax.rem(b + o, gy), lax.rem(b + (gy - o), gy)).wait_recv()
        gathered = allbuf[t].astype(F32).reshape(kd, nv).astype(BF16)
        dst[...] += dot(acmat[...], gathered)

        def done():
            for o in range(1, gx):
                stage1(o, lax.rem(a + o, gx), a).wait_send()
            for o in range(1, gy):
                stage2(o, lax.rem(b + o, gy), b).wait_send()

        finish.append(done)

        return gathered

    gathered = correct(0, res_v, mid, wait_margins)
    gather(1, mid)
    wait_margins = start_margins(1)
    sol_ref[...] = xs[...] + dot(cmat[:own, :], gathered)
    gathered = correct(1, mid, fin_ref, wait_margins)
    sol_ref[...] += xs[...] + dot(cmat[:own, :], gathered)
    for end in finish:
        end()


def solution(mesh):
    gx, gy = mesh.shape["gx"], mesh.shape["gy"]

    def per_device(residual, stiffness, local_inverse, coarse_basis, coarse_rows, send_rows, partition_map):
        comps, cx, cy, nv = residual.shape
        own, layer = comps * cx * cy, cx * cy
        m = local_inverse.shape[-1]
        ov = send_rows.shape[-1]
        kw, kd = coarse_rows.shape[-2:]
        halo = comps * max(cx, cy)
        lanes = -(-5 * kw // 128) * 128
        vm = pl.BlockSpec(memory_space=pltpu.VMEM)
        anywhere = pl.BlockSpec(memory_space=pl.ANY)
        dma = pltpu.SemaphoreType.DMA
        out = pl.pallas_call(
            functools.partial(kernel, gx, gy, (comps, cx, cy, nv)),
            out_shape=[pltpu.VMEM((own, nv), F32)] * 2,
            in_specs=[anywhere] * 7,
            out_specs=[vm, vm],
            scratch_shapes=[
                pltpu.VMEM((own, nv), F32),
                pltpu.VMEM((cx, cy), F32),
                pltpu.VMEM((m, m), BF16),
                pltpu.VMEM((kw, m), BF16),
                pltpu.VMEM((kw, kd), BF16),
                pltpu.VMEM((4, ov), jnp.int32),
                pltpu.VMEM((1, gx * gy), jnp.int32),
                pltpu.VMEM((2, m, nv), BF16),
                pltpu.VMEM((own, 4 * ov), BF16),
                pltpu.VMEM((4 * ov, own), BF16),
                pltpu.VMEM((2, 4 * ov, nv), BF16),
                pltpu.VMEM((2, 4 * ov, nv), BF16),
                pltpu.VMEM((2, 4 * ov, nv), BF16),
                pltpu.VMEM((2, 4, halo, nv), BF16),
                pltpu.VMEM((2, 4, halo, nv), BF16),
                pltpu.VMEM((2, gy, gx, kw, nv), BF16),
                pltpu.VMEM((lanes, kd), F32),
                pltpu.VMEM((kw, m - own), F32),
                pltpu.VMEM((4 * kw, m - own), F32),
                pltpu.VMEM((own, lanes), F32),
                pltpu.VMEM((own + 4 * halo, kd), BF16),
                pltpu.VMEM((own, kd), BF16),
                pltpu.VMEM((4 * halo, kd), BF16),
                pltpu.VMEM((layer, nv), F32),
                pltpu.VMEM((layer, nv), F32),
                pltpu.VMEM((layer, nv), F32),
                pltpu.VMEM((own, nv), F32),
                pltpu.VMEM((own, nv), F32),
                dma((7,)),
                dma((2, 3, 4)),
                dma((2, 3, 4)),
                dma((3, 4)),
                dma((3, 4)),
                dma((2, gx)),
                dma((2, gx)),
                dma((2, gy)),
                dma((2, gy)),
            ],
            compiler_params=pltpu.CompilerParams(collective_id=0, has_side_effects=True),
        )(
            residual.reshape(own, nv),
            stiffness,
            local_inverse[0, 0],
            coarse_basis[0, 0],
            coarse_rows[0, 0],
            send_rows[0, 0],
            partition_map.reshape(1, -1),
        )
        return tuple(o.reshape(residual.shape) for o in out)

    placed = (
        P(None, "gx", "gy", None),
        P("gx", "gy"),
        P("gx", "gy", None, None),
        P("gx", "gy", None, None),
        P("gx", "gy", None, None),
        P("gx", "gy", None, None),
        P(),
    )
    return jax.shard_map(
        per_device,
        mesh=mesh,
        in_specs=placed,
        out_specs=(P(None, "gx", "gy", None), P(None, "gx", "gy", None)),
        check_vma=False,
    )
```

```python
import functools

import jax
import jax.numpy as jnp
from jax import lax
from jax.experimental import pallas as pl
from jax.experimental.pallas import tpu as pltpu
from jax.sharding import PartitionSpec as P

MESH = pl.DeviceIdType.MESH
F32 = jnp.float32
BF16 = jnp.bfloat16
HIGH = lax.Precision.HIGHEST


def dot(x, y, **kw):
    return jnp.dot(x, y, preferred_element_type=F32, **kw)


def tdot(x, y):
    return lax.dot_general(x, y, (((0,), (0,)), ((), ())), preferred_element_type=F32)


def fiota(shape, axis):
    return lax.broadcasted_iota(jnp.int32, shape, axis).astype(F32)


def fdiv(x, n):
    return jnp.floor((x + 0.5) * (1.0 / n))


def kernel(
    gx, gy, dims,
    res_hbm, stiff_hbm, inv_hbm, basis_hbm, crows_hbm, lists_hbm, pmap_hbm,
    sol_ref, fin_ref,
    res_v, stiff_ref, inv_v, basis_ref, crows_ref, lists_ref, pmap_ref, sub, sel, selt, outs, backs, backr, hs, hr, allbuf,
    sext, bsend, brecv, bextf, cmat, acmat, csend, diag, m_lo, m_hi, xs, mid,
    lsem, nsem_s, nsem_r, csem_s, csem_r, g1s, g1r, g2s, g2r,
):
    comps, cx, cy, nv = dims
    halo = hr.shape[2]
    hrows = (comps * cy, comps * cy, comps * cx, comps * cx)
    own = comps * cx * cy
    layer = cx * cy
    ov = lists_ref.shape[1]
    kw, kd = crows_ref.shape
    a = lax.axis_index("gx")
    b = lax.axis_index("gy")

    wanted = [
        (lists_hbm, lists_ref), (res_hbm, res_v), (pmap_hbm, pmap_ref), (crows_hbm, crows_ref),
        (basis_hbm, basis_ref), (stiff_hbm, stiff_ref), (inv_hbm, inv_v),
    ]
    loads = [pltpu.make_async_copy(x, y, lsem.at[k]) for k, (x, y) in enumerate(wanted)]
    load_lists, load_res, load_pmap, load_crows, load_basis, load_stiff, load_inv = loads
    barrier = pltpu.get_barrier_semaphore()
    for o in range(1, gx):
        pl.semaphore_signal(barrier, inc=1, device_id=(lax.rem(a + o, gx), b), device_id_type=MESH)
    for o in range(1, gy):
        pl.semaphore_signal(barrier, inc=1, device_id=(a, lax.rem(b + o, gy)), device_id_type=MESH)

    for load in loads:
        load.start()

    up = [(a + 1, b), (a - 1, b), (a, b + 1), (a, b - 1)]
    has_up = [a < gx - 1, a > 0, b < gy - 1, b > 0]
    down = [up[p ^ 1] for p in range(4)]
    has_down = [has_up[p ^ 1] for p in range(4)]
    finish = []

    def send(copies, conds, wait):
        for p in (2, 3, 0, 1):
            @pl.when(conds[p])
            def _(p=p):
                for c in copies(p):
                    getattr(c, wait)()

    def trade(copies, forward):
        to, fro = (has_up, has_down) if forward else (has_down, has_up)
        send(copies, to, "start")
        finish.append(lambda: send(copies, to, "wait_send"))
        return lambda: send(copies, fro, "wait_recv")

    def remote(src, dst, s, r, dev):
        return pltpu.make_async_remote_copy(
            src_ref=src, dst_ref=dst, send_sem=s, recv_sem=r, device_id=dev, device_id_type=MESH
        )

    load_lists.wait()
    rows = fiota((own, ov), 0)
    lists = lists_ref[...].astype(F32)
    for h in range(2):
        two = [jnp.where(rows == lists[p ^ 1 : (p ^ 1) + 1], 1.0, 0.0) for p in (2 * h, 2 * h + 1)]
        both = jnp.concatenate(two, axis=1)
        sel[:, 2 * ov * h : 2 * ov * (h + 1)] = both.astype(BF16)
        selt[2 * ov * h : 2 * ov * (h + 1), :] = both.T.astype(BF16)

    for p in range(4):
        at = own + p * ov

        @pl.when(jnp.logical_not(has_down[p]))
        def _(p=p, at=at):
            for t in range(2):
                sub[t, at : at + ov, :] = jnp.zeros((ov, nv), BF16)
                hr[t, p] = jnp.zeros(hr.shape[2:], BF16)

        @pl.when(jnp.logical_not(has_up[p]))
        def _(p=p):
            for t in range(2):
                backr[t, p * ov : (p + 1) * ov, :] = jnp.zeros((ov, nv), BF16)
            sext[(p + 1) * kw : (p + 2) * kw, :] = jnp.zeros((kw, kd), F32)
            brecv[p * kw : (p + 1) * kw, :] = jnp.zeros((kw, 4 * ov), F32)

        @pl.when(jnp.logical_not(has_down[p]))
        def _(p=p):
            cmat[own + p * halo : own + (p + 1) * halo, :] = jnp.zeros((halo, kd), BF16)

    sext[5 * kw :, :] = jnp.zeros((sext.shape[0] - 5 * kw, kd), F32)

    load_res.wait()

    def gather(t, src):
        value = src[...].astype(BF16)
        sub[t, :own, :] = value
        outs[t] = dot(selt[...], value).astype(BF16)

    gather(0, res_v)
    pl.semaphore_wait(barrier, gx + gy - 2)

    def start_margins(t):
        return trade(
            lambda p: [remote(outs.at[t, pl.ds(p * ov, ov)], sub.at[t, pl.ds(own + p * ov, ov)],
                              nsem_s.at[t, 0, p], nsem_r.at[t, 0, p], up[p])],
            True,
        )

    wait_margins = start_margins(0)

    load_pmap.wait()
    load_crows.wait()
    load_basis.wait()
    wide = min(kd, 256)
    n = gx * gy
    pmf = jnp.broadcast_to(pmap_ref[...].astype(F32), (8, n))

    def order(c, _):
        q = fiota((1, wide), 1) + (c * wide).astype(F32)
        slot = fdiv(q, kw)
        slab = fdiv(slot, gx)
        dev = (slot - slab * gx) * gy + slab
        pick = jnp.where(fiota((n, wide), 0) == dev, 1.0, 0.0)
        place = dot(pmf, pick, precision=HIGH)[0:1] * kw + (q - slot * kw)
        perm = jnp.where(fiota((kd, wide), 0) == place, 1.0, 0.0).astype(BF16)
        sext[0:kw, pl.ds(pl.multiple_of(c * wide, wide), wide)] = dot(crows_ref[...], perm)
        return 0

    lax.fori_loop(jnp.int32(0), jnp.int32(kd // wide), order, 0)
    bsend[...] = basis_ref[:, own:].astype(F32)
    wait_coarse = trade(
        lambda p: [
            remote(sext.at[pl.ds(0, kw)], sext.at[pl.ds((p + 1) * kw, kw)], csem_s.at[0, p], csem_r.at[0, p], down[p]),
            remote(bsend, brecv.at[pl.ds(p * kw, kw)], csem_s.at[1, p], csem_r.at[1, p], down[p]),
        ],
        False,
    )

    load_stiff.wait()
    r1 = fiota((layer, cy), 0)
    first = fdiv(r1, cy)
    mine = jnp.where(fiota((layer, cx), 1) == fdiv(fiota((layer, cx), 0), cy), 1.0, 0.0)
    spread = dot(mine, stiff_ref[...], precision=HIGH)
    spread = jnp.where(fiota((layer, cy), 1) == r1 - first * cy, spread, 0.0)
    diag[...] = jnp.broadcast_to(4.0 + jnp.sum(spread, axis=1, keepdims=True), (layer, nv))
    rr = fiota((layer, nv), 0)
    second = rr - fdiv(rr, cy) * cy
    m_lo[...] = jnp.where(second == 0.0, 0.0, 1.0)
    m_hi[...] = jnp.where(second == cy - 1.0, 0.0, 1.0)

    def layer_rows(ref, p):
        if p >= 2:
            return ref[pl.ds((cy - 1) * (3 - p), comps * cx, stride=cy), :]
        skip = (layer - cy) * (1 - p)
        return jnp.concatenate([ref[c * layer + skip : c * layer + skip + cy, :] for c in range(comps)], axis=0)

    def operate(x_ref, dst, src):
        zero = jnp.zeros((cy, nv), F32)
        for c in range(comps):
            at = pl.ds(c * layer, layer)
            x = x_ref[at, :]
            beside = jnp.concatenate([zero, x[:-cy]], axis=0) + jnp.concatenate([x[cy:], zero], axis=0)
            beside += pltpu.roll(x, 1, 0) * m_lo[...] + pltpu.roll(x, layer - 1, 0) * m_hi[...]
            value = beside - diag[...] * x
            dst[at, :] = value if src is None else src[at, :] + value

    def add_layers(dst, around):
        for c in range(comps):
            base = c * layer
            dst[base : base + cy, :] += around(0)[c * cy : (c + 1) * cy]
            dst[base + layer - cy : base + layer, :] += around(1)[c * cy : (c + 1) * cy]
        low = pl.ds(0, comps * cx, stride=cy)
        high = pl.ds(cy - 1, comps * cx, stride=cy)
        dst[low, :] = dst[low, :] + around(2)
        dst[high, :] = dst[high, :] + around(3)

    wait_edges = []

    def correct(t, src, dst, wait_margins):
        if t == 0:
            load_inv.wait()
        part = dot(inv_v[:, :own], sub[t, :own, :])
        cpart = dot(basis_ref[:, :own], sub[t, :own, :])
        wait_margins()
        edge = sub[t, own:, :]
        cin = cpart + dot(basis_ref[:, own:], edge)
        allbuf[t, b, a] = cin.astype(BF16)

        def stage1(o, dev, slot):
            ref = allbuf.at[t, b, slot]
            return remote(ref, ref, g1s.at[t, o], g1r.at[t, o], (dev, b))

        def stage2(o, dev, slot):
            ref = allbuf.at[t, slot]
            return remote(ref, ref, g2s.at[t, o], g2r.at[t, o], (a, dev))

        for o in range(1, gx):
            stage1(o, lax.rem(a + o, gx), a).start()
        backs[t] = (part[own:] + dot(inv_v[own:, own:], edge)).astype(BF16)
        wait_back = trade(
            lambda p: [remote(backs.at[t, pl.ds(p * ov, ov)], backr.at[t, pl.ds(p * ov, ov)],
                              nsem_s.at[t, 1, p], nsem_r.at[t, 1, p], down[p])],
            False,
        )
        xs[...] = part[:own] + dot(inv_v[:own, own:], edge)
        if t == 0:
            wait_coarse()
            rb = fdiv(fiota((4 * kw, 4 * ov), 0), kw)
            cb = fdiv(fiota((4 * kw, 4 * ov), 1), ov)
            margins = jnp.where(rb == cb, brecv[...], 0.0).astype(BF16)
            below = dot(margins, selt[...])
            rest = jnp.zeros((sext.shape[0] - 5 * kw, own), F32)
            ext = jnp.concatenate([basis_ref[:, :own].astype(F32), below, rest], axis=0)
            bextf[...] = ext.T
            edges = jnp.concatenate([layer_rows(bextf, p) for p in range(4)], axis=0).astype(BF16)

            def build(c, _):
                at = pl.ds(pl.multiple_of(c * wide, wide), wide)
                part_s = sext[:, at].astype(BF16)
                csend[:, at] = dot(edges, part_s).astype(BF16)
                return 0

            lax.fori_loop(jnp.int32(0), jnp.int32(kd // wide), build, 0)
            wait_edges.append(trade(
                lambda p: [remote(csend.at[pl.ds(p * halo, halo)], cmat.at[pl.ds(own + p * halo, halo)],
                                  csem_s.at[2, p], csem_r.at[2, p], up[p])],
                True,
            ))
        for o in range(1, gx):
            stage1(o, lax.rem(a + o, gx), lax.rem(a + (gx - o), gx)).wait_recv()
        for o in range(1, gy):
            stage2(o, lax.rem(b + o, gy), b).start()
        wait_back()
        xs[...] += dot(sel[...], backr[t])

        for p in range(4):
            hs[t, p, : hrows[p], :] = layer_rows(xs, p).astype(hs.dtype)
        wait_halo = trade(
            lambda p: [remote(hs.at[t, p], hr.at[t, p], nsem_s.at[t, 2, p], nsem_r.at[t, 2, p], up[p])],
            True,
        )
        operate(xs, dst, src)
        if t == 0:
            wait_edges[0]()
            bext = bextf[...].astype(BF16)

            def fill(c, _):
                at = pl.ds(pl.multiple_of(c * nv, nv), nv)
                value = dot(bext, sext[:, at].astype(BF16))
                cmat[:own, at] = value.astype(BF16)
                sol_ref[...] = value
                operate(sol_ref, fin_ref, None)
                add_layers(fin_ref, lambda p: cmat[own + p * halo : own + p * halo + hrows[p], at].astype(F32))
                acmat[:, at] = fin_ref[...].astype(BF16)
                return 0

            lax.fori_loop(jnp.int32(0), jnp.int32(kd // nv), fill, 0)
        wait_halo()
        add_layers(dst, lambda p: hr[t, p, : hrows[p], :].astype(F32))
        for o in range(1, gy):
            stage2(o, lax.rem(b + o, gy), lax.rem(b + (gy - o), gy)).wait_recv()
        gathered = allbuf[t].astype(F32).reshape(kd, nv).astype(BF16)
        dst[...] += dot(acmat[...], gathered)

        def done():
            for o in range(1, gx):
                stage1(o, lax.rem(a + o, gx), a).wait_send()
            for o in range(1, gy):
                stage2(o, lax.rem(b + o, gy), b).wait_send()

        finish.append(done)

        return gathered

    gathered = correct(0, res_v, mid, wait_margins)
    gather(1, mid)
    wait_margins = start_margins(1)
    sol_ref[...] = xs[...] + dot(cmat[:own, :], gathered)
    gathered = correct(1, mid, fin_ref, wait_margins)
    sol_ref[...] += xs[...] + dot(cmat[:own, :], gathered)
    for end in finish:
        end()


def solution(mesh):
    gx, gy = mesh.shape["gx"], mesh.shape["gy"]

    def per_device(residual, stiffness, local_inverse, coarse_basis, coarse_rows, send_rows, partition_map):
        comps, cx, cy, nv = residual.shape
        own, layer = comps * cx * cy, cx * cy
        m = local_inverse.shape[-1]
        ov = send_rows.shape[-1]
        kw, kd = coarse_rows.shape[-2:]
        halo = comps * max(cx, cy)
        lanes = -(-5 * kw // 128) * 128
        vm = pl.BlockSpec(memory_space=pltpu.VMEM)
        anywhere = pl.BlockSpec(memory_space=pl.ANY)
        dma = pltpu.SemaphoreType.DMA
        out = pl.pallas_call(
            functools.partial(kernel, gx, gy, (comps, cx, cy, nv)),
            out_shape=[pltpu.VMEM((own, nv), F32)] * 2,
            in_specs=[anywhere] * 7,
            out_specs=[vm, vm],
            scratch_shapes=[
                pltpu.VMEM((own, nv), F32),
                pltpu.VMEM((cx, cy), F32),
                pltpu.VMEM((m, m), BF16),
                pltpu.VMEM((kw, m), BF16),
                pltpu.VMEM((kw, kd), BF16),
                pltpu.VMEM((4, ov), jnp.int32),
                pltpu.VMEM((1, gx * gy), jnp.int32),
                pltpu.VMEM((2, m, nv), BF16),
                pltpu.VMEM((own, 4 * ov), BF16),
                pltpu.VMEM((4 * ov, own), BF16),
                pltpu.VMEM((2, 4 * ov, nv), BF16),
                pltpu.VMEM((2, 4 * ov, nv), BF16),
                pltpu.VMEM((2, 4 * ov, nv), BF16),
                pltpu.VMEM((2, 4, halo, nv), BF16),
                pltpu.VMEM((2, 4, halo, nv), BF16),
                pltpu.VMEM((2, gy, gx, kw, nv), BF16),
                pltpu.VMEM((lanes, kd), F32),
                pltpu.VMEM((kw, m - own), F32),
                pltpu.VMEM((4 * kw, m - own), F32),
                pltpu.VMEM((own, lanes), F32),
                pltpu.VMEM((own + 4 * halo, kd), BF16),
                pltpu.VMEM((own, kd), BF16),
                pltpu.VMEM((4 * halo, kd), BF16),
                pltpu.VMEM((layer, nv), F32),
                pltpu.VMEM((layer, nv), F32),
                pltpu.VMEM((layer, nv), F32),
                pltpu.VMEM((own, nv), F32),
                pltpu.VMEM((own, nv), F32),
                dma((7,)),
                dma((2, 3, 4)),
                dma((2, 3, 4)),
                dma((3, 4)),
                dma((3, 4)),
                dma((2, gx)),
                dma((2, gx)),
                dma((2, gy)),
                dma((2, gy)),
            ],
            compiler_params=pltpu.CompilerParams(collective_id=0, has_side_effects=True),
        )(
            residual.reshape(own, nv),
            stiffness,
            local_inverse[0, 0],
            coarse_basis[0, 0],
            coarse_rows[0, 0],
            send_rows[0, 0],
            partition_map.reshape(1, -1),
        )
        return tuple(o.reshape(residual.shape) for o in out)

    placed = (
        P(None, "gx", "gy", None),
        P("gx", "gy"),
        P("gx", "gy", None, None),
        P("gx", "gy", None, None),
        P("gx", "gy", None, None),
        P("gx", "gy", None, None),
        P(),
    )
    return jax.shard_map(
        per_device,
        mesh=mesh,
        in_specs=placed,
        out_specs=(P(None, "gx", "gy", None), P(None, "gx", "gy", None)),
        check_vma=False,
    )
```
